32 devices in a mesh: clip: 8 (over z, x), cap: 4 (over y, core).
Axes of the slice: x: 2, y: 2, z: 4, core: 2. Of those that a mesh axis runs over, the one named last changes fastest.
Arguments:
- text: bfloat16 [128, 512], replicated, may hold values from -8 to 8
- patches: bfloat16 [16, 16, 196, 512], P('clip', None, 'cap'), may hold values from -6 to 6
- frame_slots: int32 [16, 16], P('clip'), may hold values from -1 to 127, as said below
Outputs:
- contrast_loss: float32 [], replicated
- patch_grad: bfloat16 [16, 16, 196, 512], P('clip', None, 'cap')
- text_grad: float32 [128, 512], P(('clip', 'cap'))
The draws below stay inside these ranges and needn't reach their ends.
Inputs may be any that keep to these rules, and one draw needn't show every extreme that they name: `frame_slots`: in every clip the valid frames are the first 4 to 16 slots, and on some index of clip every clip has all 16; all clips together have 16 * 8 valid frames. A valid entry is t * 16 + s: the frame goes to index t of clip, slot s; every index of clip receives exactly 16 frames, one in each slot. A frame stays on its own index of clip unless that index holds more than 16 frames; then its frames past the first 16, in clip and frame order, go to other indices. At most 3 frames go from one index of clip to another, a bound that some pair reaches.
All inputs are finite; a program needn't handle non-finite values.
Results may differ from the reference program's by a relative error of at most 0.0065.
Values may be sent and summed in bfloat16 or wider, within the bound.
No kernel may reach another device: no remote copies, remote signals or barrier semaphores. Data moves between devices by JAX's collectives and lax.ppermute only.
A program may use at most 64 MiB of HBM per device.

```python
import jax
import jax.numpy as jnp
from jax import lax

D = 512
PATCHES = 196
WORDS = 8
FMAX = 16
MEANF = 8
CLIP_DEV = 2
CLIPS = 16
SLOTS = 16


def draw_text(key, part):
    values = jax.random.truncated_normal(jax.random.fold_in(key, 1), -4.0, 4.0, (CLIPS * WORDS, D), jnp.float32)
    return values.astype(jnp.bfloat16)


def draw_patches(key, part):
    values = jax.random.truncated_normal(jax.random.fold_in(key, 3), -4.0, 4.0, (CLIPS, FMAX, PATCHES, D), jnp.float32)
    return values.astype(jnp.bfloat16)


def fill_greedy(total, proposed, ceiling):
    before = jnp.cumsum(proposed) - proposed
    first_pass = jnp.clip(total - before, 0, proposed)
    leftover = total - jnp.sum(first_pass)
    headroom = ceiling - first_pass
    before_room = jnp.cumsum(headroom) - headroom
    second_pass = jnp.clip(leftover - before_room, 0, headroom)
    return first_pass + second_pass


def draw_frame_slots(key, part):
    subkeys = jax.random.split(jax.random.fold_in(key, 57), 6)
    devices = CLIPS // CLIP_DEV
    excess = CLIP_DEV * (FMAX - MEANF)
    room_most = max(2, (excess + devices - 2) // (devices - 1))
    device_index = jnp.arange(devices, dtype=jnp.int32)
    full_device = jax.random.randint(subkeys[0], (), 0, devices)
    empty_device = (full_device + 1 + jax.random.randint(subkeys[1], (), 0, devices - 1)) % devices
    is_full = device_index == full_device
    is_empty = device_index == empty_device
    others = jnp.logical_not(is_full | is_empty).astype(jnp.int32)
    extra = (devices - 1) * room_most - excess
    shuffle = jax.random.permutation(subkeys[2], devices)
    proposed_add = jax.random.randint(subkeys[3], (devices,), 0, room_most + 1) * others
    added_order = fill_greedy(extra, proposed_add[shuffle], room_most * others[shuffle])
    added = jnp.zeros((devices,), jnp.int32).at[shuffle].set(added_order)
    totals = jnp.where(is_full, CLIP_DEV * FMAX, SLOTS - room_most + added)
    clip_extra = jax.random.randint(subkeys[4], (devices, CLIP_DEV), 0, FMAX - 3)
    split = jax.vmap(fill_greedy, in_axes=(0, 0, None))(totals - 4 * CLIP_DEV, clip_extra, FMAX - 4)
    frames = (4 + split).reshape(CLIPS)
    present = jnp.arange(FMAX, dtype=jnp.int32)[None, :] < frames[:, None]
    ranks = jnp.cumsum(present.reshape(devices, CLIP_DEV * FMAX).astype(jnp.int32), axis=1) - 1
    ranks = ranks.reshape(CLIPS, FMAX)
    owner = (jnp.arange(CLIPS, dtype=jnp.int32) // CLIP_DEV)[:, None]
    home = ranks < SLOTS
    room = SLOTS - jnp.minimum(totals, SLOTS)
    mixing = jax.random.permutation(subkeys[5], devices)
    place = jnp.zeros((devices,), jnp.int32).at[mixing].set(device_index)
    receive_order = jnp.argsort(jnp.where(is_empty, -1, place), stable=True)
    room_ordered = room[receive_order]
    start_ordered = jnp.cumsum(room_ordered) - room_ordered
    room_start = jnp.zeros((devices,), jnp.int32).at[receive_order].set(start_ordered)
    beyond = ranks - SLOTS
    hit = (beyond[:, :, None] >= room_start[None, None, :]) & (beyond[:, :, None] < (room_start + room)[None, None, :])
    receiver = jnp.sum(jnp.where(hit, device_index[None, None, :], 0), axis=2)
    far_slot = totals[receiver] + beyond - room_start[receiver]
    target = jnp.where(home, owner, receiver)
    slot = jnp.where(home, ranks, far_slot)
    return jnp.where(present, target * SLOTS + slot, -1)


def setup_inputs(seed: int = 0) -> dict:
    arg_keys = jax.random.split(jax.random.key(seed), 4)
    text = draw_text(jax.random.fold_in(arg_keys[3], 71), 0)
    patches = draw_patches(jax.random.fold_in(arg_keys[3], 71), 0)
    frame_slots = draw_frame_slots(jax.random.fold_in(arg_keys[3], 71), 0)
    return dict(text=text, patches=patches, frame_slots=frame_slots)


logit_scale = 32.0
loss_scale = 8192.0
big_value = 1e30


def frame_scores(text, frames):
    flattened = frames.reshape(-1, frames.shape[-1])
    scores = lax.dot_general(text, flattened, (((1,), (1,)), ((), ())), preferred_element_type=jnp.float32)
    return scores * (D ** -0.5)


def usable_columns(slot_row):
    return jnp.repeat(slot_row >= 0, PATCHES)[None, :]


def pool_clip(text, frames, slot_row):
    scores = frame_scores(text, frames)
    usable = usable_columns(slot_row)
    maximum = jnp.max(jnp.where(usable, scores, -big_value), axis=1)
    weight = jnp.where(usable, jnp.exp(scores - maximum[:, None]), 0.0)
    totals = jnp.sum(weight, axis=1)
    pooled = jnp.sum(weight * scores, axis=1) / totals
    return maximum, totals, pooled


def reference(text, patches, frame_slots):
    maxima, sums, pooled = lax.map(lambda element: pool_clip(text, element[0], element[1]), (patches, frame_slots))
    similar = jnp.mean(pooled.reshape(CLIPS, CLIPS, WORDS), axis=2)
    logits = logit_scale * similar.T
    row_terms = jax.nn.logsumexp(logits, axis=1)
    col_terms = jax.nn.logsumexp(logits, axis=0)
    matched = jnp.diagonal(logits)
    contrast_loss = 0.5 * (jnp.mean(row_terms - matched) + jnp.mean(col_terms - matched))
    identity = jnp.eye(CLIPS, dtype=logits.dtype)
    grad_logits = (loss_scale * 0.5 / CLIPS) * (jax.nn.softmax(logits, axis=1) + jax.nn.softmax(logits, axis=0) - 2.0 * identity)
    grad_pooled = jnp.repeat((logit_scale / WORDS) * grad_logits.T, WORDS, axis=1)

    def backward(running, element):
        frames, slot_row, maximum, totals, pool_row, grad_row = element
        scores = frame_scores(text, frames)
        usable = usable_columns(slot_row)
        weights = jnp.where(usable, jnp.exp(scores - maximum[:, None]) / totals[:, None], 0.0)
        grad_scores = (grad_row[:, None] * weights * (1.0 + scores - pool_row[:, None])).astype(jnp.bfloat16)
        grad_frames = lax.dot_general(grad_scores, text, (((0,), (0,)), ((), ())), preferred_element_type=jnp.float32) * (D ** -0.5)
        flattened = frames.reshape(-1, frames.shape[-1])
        running = running + lax.dot_general(grad_scores, flattened, (((1,), (0,)), ((), ())), preferred_element_type=jnp.float32) * (D ** -0.5)
        return running, grad_frames.astype(jnp.bfloat16).reshape(frames.shape)

    text_grad, patch_grad = lax.scan(backward, jnp.zeros(text.shape, jnp.float32), (patches, frame_slots, maxima, sums, pooled, grad_pooled))
    return contrast_loss, patch_grad, text_grad
```

```python
import jax
import jax.numpy as jnp
from jax import lax
from jax.sharding import PartitionSpec as P

WORDS = 8
AXES = ("clip", "cap")

logit_scale = 32.0
loss_scale = 8192.0
big_value = 1e30


def per_device(text, patches, frame_slots):
    clip_devices = lax.axis_size("clip")
    cap_devices = lax.axis_size("cap")
    devices = clip_devices * cap_devices
    my_rank = lax.axis_index("clip")
    local_clips, frame_max, patch_rows, width = patches.shape
    text_rows = text.shape[0]
    clip_total = clip_devices * local_clips
    captions = text_rows // WORDS
    factor_scale = width ** (-0.5)
    columns = patch_rows * frame_max

    flat = patches.transpose(0, 2, 1, 3).reshape(local_clips * columns, width)
    usable = jnp.broadcast_to((frame_slots >= 0)[:, None, :], (local_clips, patch_rows, frame_max))
    usable = usable.reshape(local_clips, columns, 1)

    scores = lax.dot_general(
        flat, text, (((1,), (1,)), ((), ())), preferred_element_type=jnp.float32
    ) * factor_scale
    scores = scores.reshape(local_clips, columns, text_rows)
    maximum = jnp.max(jnp.where(usable, scores, -big_value), axis=1)
    weight = jnp.where(usable, jnp.exp(scores - maximum[:, None, :]), 0.0)
    total = jnp.sum(weight, axis=1)
    numerator = jnp.sum(weight * scores, axis=1)

    partial = jnp.concatenate([maximum, total, numerator], axis=0)
    sent = jnp.broadcast_to(partial[None], (devices,) + partial.shape)
    got = lax.all_to_all(sent, AXES, split_axis=0, concat_axis=0, tiled=True)
    got = got.reshape(clip_devices, cap_devices, 3, local_clips, text_rows)
    maxima, totals, numerators = got[:, :, 0], got[:, :, 1], got[:, :, 2]
    merged_max = jnp.max(maxima, axis=1)
    factor = jnp.exp(maxima - merged_max[:, None])
    merged_sum = jnp.sum(factor * totals, axis=1)
    merged_num = jnp.sum(factor * numerators, axis=1)
    all_max = merged_max.reshape(clip_total, text_rows)
    all_sum = merged_sum.reshape(clip_total, text_rows)
    all_pool = (merged_num / merged_sum).reshape(clip_total, text_rows)

    by_clip = logit_scale * jnp.mean(all_pool.reshape(clip_total, captions, WORDS), axis=2)
    row_max = jnp.max(by_clip, axis=0, keepdims=True)
    row_exp = jnp.exp(by_clip - row_max)
    row_sum = jnp.sum(row_exp, axis=0, keepdims=True)
    col_max = jnp.max(by_clip, axis=1, keepdims=True)
    col_exp = jnp.exp(by_clip - col_max)
    col_sum = jnp.sum(col_exp, axis=1, keepdims=True)
    identity = jnp.eye(clip_total, dtype=jnp.float32)
    grad_logits = (loss_scale * 0.5 / clip_total) * (
        row_exp / row_sum + col_exp / col_sum - 2.0 * identity
    )
    grad_pooled = jnp.repeat(logit_scale / WORDS * grad_logits, WORDS, axis=1)
    matched = jnp.sum(identity * by_clip)
    contrast_loss = 0.5 / clip_total * (
        jnp.sum(row_max + jnp.log(row_sum)) + jnp.sum(col_max + jnp.log(col_sum)) - 2.0 * matched
    )

    first_clip = my_rank * local_clips

    def own(rows):
        return lax.dynamic_slice_in_dim(rows, first_clip, local_clips, 0)[:, None, :]

    weights = jnp.where(usable, jnp.exp(scores - own(all_max)) / own(all_sum), 0.0)
    grad_scores = (own(grad_pooled) * weights * (1.0 + scores - own(all_pool))).astype(jnp.bfloat16)
    grad_flat = grad_scores.reshape(local_clips * columns, text_rows)
    text_part = lax.dot_general(
        grad_flat, flat, (((0,), (0,)), ((), ())), preferred_element_type=jnp.float32
    )
    text_sent = (text_part * factor_scale).reshape(devices, text_rows // devices, width)
    text_got = lax.all_to_all(text_sent, AXES, split_axis=0, concat_axis=0, tiled=True)
    text_grad = jnp.sum(text_got, axis=0)
    frame_grad = lax.dot_general(
        grad_flat, text, (((1,), (0,)), ((), ())), preferred_element_type=jnp.float32
    )
    frame_grad = (frame_grad * factor_scale).astype(jnp.bfloat16)
    frame_grad = frame_grad.reshape(local_clips, patch_rows, frame_max, width).transpose(0, 2, 1, 3)
    return (contrast_loss, frame_grad, text_grad)


def solution(mesh):
    return jax.shard_map(
        per_device,
        mesh=mesh,
        in_specs=(P(), P("clip", None, "cap", None), P("clip", None)),
        out_specs=(P(), P("clip", None, "cap", None), P(AXES, None)),
        check_vma=False,
    )
```

```python
import functools

import jax
import jax.numpy as jnp
from jax import lax
from jax.experimental import pallas as pl
from jax.experimental.pallas import tpu as pltpu
from jax.sharding import PartitionSpec as P

WORDS = 8
AXES = ("clip", "cap")

logit_scale = 32.0
loss_scale = 8192.0
big_value = 1e30

F32 = jnp.float32
BF16 = jnp.bfloat16
ANY = pl.BlockSpec(memory_space=pl.ANY)
VMEM = pl.BlockSpec(memory_space=pltpu.VMEM)


FORWARD_PARTS = 1
BACKWARD_PARTS = 2


def row_parts(columns, frame_max, parts):
    patch_rows = columns // frame_max
    edges = [patch_rows * k // parts * frame_max for k in range(parts + 1)]
    return [(a, b - a) for a, b in zip(edges, edges[1:])]


def valid_mask(slots_ref, v, frame_max, lanes):
    count = jnp.int32(0)
    for f in range(frame_max):
        count += (slots_ref[v, f] >= 0).astype(jnp.int32)
    return lax.broadcasted_iota(jnp.int32, (1, frame_max, lanes), 1) < count


def forward_kernel(
    clips, frame_max, scale,
    text_hbm, flat_hbm, slots_hbm,
    stats_ref, scores_ref, flat_ref, text_ref,
    slots_ref, sems,
):
    columns = flat_ref.shape[0] // clips
    lanes = text_ref.shape[0]
    parts = row_parts(columns, frame_max, FORWARD_PARTS)
    runs = [pl.ds(v * columns + start, size) for v in range(clips) for start, size in parts]
    copies = [
        pltpu.make_async_copy(flat_hbm.at[run], flat_ref.at[run], sems.at[k])
        for k, run in enumerate(runs)
    ]
    text_copy = pltpu.make_async_copy(text_hbm, text_ref, sems.at[len(runs)])
    slots_copy = pltpu.make_async_copy(slots_hbm, slots_ref, sems.at[len(runs) + 1])
    text_copy.start()
    slots_copy.start()
    for copy in copies:
        copy.start()
    slots_copy.wait()
    masks = [valid_mask(slots_ref, v, frame_max, lanes) for v in range(clips)]
    text_copy.wait()
    for v in range(clips):
        peak = jnp.full((frame_max, lanes), -big_value, F32)
        for k in range(v * len(parts), (v + 1) * len(parts)):
            copies[k].wait()
            part = lax.dot_general(
                flat_ref[runs[k]], text_ref[...], (((1,), (1,)), ((), ())),
                preferred_element_type=F32,
            ) * scale
            part = jnp.where(masks[v], part.reshape(-1, frame_max, lanes), -big_value)
            scores_ref[runs[k]] = part.reshape(-1, lanes)
            peak = jnp.maximum(peak, jnp.max(part, axis=0))
        peak = jnp.max(peak, axis=0, keepdims=True)
        part = scores_ref[pl.ds(v * columns, columns)].reshape(-1, frame_max, lanes)
        weight = jnp.exp(part - peak[None])
        total = jnp.sum(weight, axis=0)
        weighted = jnp.sum(weight * part, axis=0)
        stats_ref[pl.ds(v, 1)] = peak
        stats_ref[pl.ds(clips + v, 1)] = jnp.sum(total, axis=0, keepdims=True)
        stats_ref[pl.ds(2 * clips + v, 1)] = jnp.sum(weighted, axis=0, keepdims=True)


def caption_mean(row, lanes):
    row = jnp.broadcast_to(row, (8, lanes))
    lane = lax.broadcasted_iota(jnp.int32, (8, lanes), 1)
    step = 1
    while step < WORDS:
        up = pltpu.roll(row, lanes - step, 1)
        down = pltpu.roll(row, step, 1)
        row = row + jnp.where((lane & step) == 0, up, down)
        step *= 2
    return row * (1.0 / WORDS)


def middle_kernel(clips, frame_max, shards, scale, *refs):
    stats = refs[:shards]
    scores_ref, flat_ref, send_ref, slopes_ref = refs[shards:]
    columns = flat_ref.shape[0] // clips
    lanes = scores_ref.shape[1]
    width = flat_ref.shape[1]
    devices, own_rows, _ = send_ref.shape
    group = WORDS // clips
    lane = lax.broadcasted_iota(jnp.int32, (8, lanes), 1)
    means = None
    for v in range(clips):
        peaks = [s[pl.ds(v, 1)] for s in stats]
        peak = functools.reduce(jnp.maximum, peaks)
        factors = [jnp.exp(p - peak) for p in peaks]
        total = sum(f * s[pl.ds(clips + v, 1)] for f, s in zip(factors, stats))
        pooled = sum(f * s[pl.ds(2 * clips + v, 1)] for f, s in zip(factors, stats)) / total
        inverse = 1.0 / total
        mean = caption_mean(pooled, lanes)
        inside = (lane & (WORDS - 1)) >= v * group
        means = mean if means is None else jnp.where(inside, mean, means)
        rows = pl.ds(v * columns, columns)
        part = scores_ref[rows].reshape(-1, frame_max, lanes)
        slope = jnp.exp(part - peak[None]) * inverse[None] * (1.0 + part - pooled[None])
        slopes_ref[rows] = slope.reshape(columns, lanes)
        grads = lax.dot_general(
            slopes_ref[rows].astype(BF16), flat_ref[rows], (((0,), (0,)), ((), ())),
            preferred_element_type=F32,
        ) * scale
        send_ref[:, :, pl.ds(v * width, width)] = grads.reshape(devices, own_rows, width).astype(BF16)
    high = means.astype(BF16)
    rest = means - high.astype(F32)
    middle = rest.astype(BF16)
    low = (rest - middle.astype(F32)).astype(BF16)
    row = lax.broadcasted_iota(jnp.int32, (own_rows, lanes), 0)
    pieces = [p.astype(F32)[:1] for p in (high, middle, low)]
    block = jnp.where(row == 0, pieces[0], jnp.where(row == 1, pieces[1], jnp.where(row == 2, pieces[2], 0.0)))
    send_ref[:, :, pl.ds(clips * width, lanes)] = jnp.broadcast_to(
        block.astype(BF16)[None], (devices, own_rows, lanes)
    )


def backward_kernel(
    clips, frame_max, shards, scale,
    got_ref, slopes_ref, text_ref,
    loss_hbm, flat_grad_hbm, text_grad_hbm,
    staged_ref, loss_ref, text_grad_ref, sems,
):
    lanes, width = text_ref.shape
    devices, own_rows, _ = got_ref.shape
    owners = devices // shards
    clip_total = owners * clips
    captions = lanes // WORDS
    group = WORDS // clips
    rank = lax.axis_index("clip")
    device = rank * shards + lax.axis_index("cap")
    lane = lax.broadcasted_iota(jnp.int32, (1, lanes), 1)
    word = lane & (WORDS - 1)
    rows = []
    for i in range(owners):
        pieces = got_ref[i * shards, :, pl.ds(clips * width, lanes)].astype(F32)
        rows.append(pieces[0:1] + pieces[1:2] + pieces[2:3])
    packed = jnp.concatenate(rows, axis=0)
    by_clip = []
    for v in range(clips):
        mean = packed
        step = group
        while step < WORDS:
            up = pltpu.roll(mean, lanes - step, 1)
            down = pltpu.roll(mean, step, 1)
            keep = ((word & step) != 0) == ((v * group & step) != 0)
            mean = jnp.where(keep, mean, jnp.where((word & step) == 0, up, down))
            step *= 2
        by_clip.append(logit_scale * mean)
    owner = lax.broadcasted_iota(jnp.int32, (owners, lanes), 0)
    caption = lax.broadcasted_iota(jnp.int32, (owners, lanes), 1) // WORDS
    row_max = functools.reduce(jnp.maximum, [jnp.max(b, axis=0, keepdims=True) for b in by_clip])
    row_exp = [jnp.exp(b - row_max) for b in by_clip]
    row_sum = sum(jnp.sum(e, axis=0, keepdims=True) for e in row_exp)
    per_word = 1.0 / WORDS
    loss = jnp.sum(row_max + jnp.log(row_sum), axis=1, keepdims=True) * per_word
    factor = logit_scale / WORDS * loss_scale * 0.5 / clip_total
    grads = []
    for v in range(clips):
        col_max = jnp.max(by_clip[v], axis=1, keepdims=True)
        col_exp = jnp.exp(by_clip[v] - col_max)
        col_sum = jnp.sum(col_exp, axis=1, keepdims=True) * per_word
        same = caption == owner * clips + v
        loss += jnp.sum(col_max + jnp.log(col_sum), axis=0, keepdims=True)
        matched = jnp.where(same, by_clip[v], 0.0)
        loss -= 2.0 * per_word * jnp.sum(jnp.sum(matched, axis=1, keepdims=True), axis=0, keepdims=True)
        grads.append(
            factor * (row_exp[v] / row_sum + col_exp / col_sum - jnp.where(same, 2.0, 0.0))
        )
    loss_ref[...] = loss * (0.5 / clip_total)
    copies = [pltpu.make_async_copy(loss_ref, loss_hbm, sems.at[0])]
    copies[0].start()

    columns = slopes_ref.shape[0] // clips
    parts = row_parts(columns, frame_max, BACKWARD_PARTS)
    for v in range(clips):
        mine = jnp.sum(jnp.where(owner == rank, grads[v], 0.0), axis=0, keepdims=True)
        for start, size in parts:
            run = pl.ds(v * columns + start, size)
            grad_scores = (slopes_ref[run] * mine).astype(BF16)
            staged_ref[run] = (
                jnp.dot(grad_scores, text_ref[...], preferred_element_type=F32) * scale
            ).astype(BF16)
            copy = pltpu.make_async_copy(
                staged_ref.at[run], flat_grad_hbm.at[run], sems.at[len(copies)]
            )
            copy.start()
            copies.append(copy)
    chosen = lax.broadcasted_iota(jnp.int32, (owners, lanes), 1) == device * own_rows
    out = jnp.zeros((own_rows, width), F32)
    for v in range(clips):
        column = jnp.sum(jnp.where(chosen, grads[v], 0.0), axis=1, keepdims=True)
        for i in range(owners):
            part = jnp.zeros((own_rows, width), F32)
            for k in range(shards):
                part += got_ref[i * shards + k, :, pl.ds(v * width, width)].astype(F32)
            out += column[i : i + 1, :] * part
    text_grad_ref[...] = out
    copies.append(pltpu.make_async_copy(text_grad_ref, text_grad_hbm, sems.at[len(copies)]))
    copies[-1].start()
    for copy in copies:
        copy.wait()


def exchange(value, axis):
    size = lax.axis_size(axis)
    got = []
    for k in range(1, size):
        if size & (size - 1) == 0:
            pairs = [(i, i ^ k) for i in range(size)]
        else:
            pairs = [(i, (i + k) % size) for i in range(size)]
        got.append(lax.ppermute(value, axis, pairs))
    return got


def far(x):
    return pltpu.with_memory_space_constraint(x, pltpu.HBM)


def per_device(text, patches, frame_slots):
    clip_devices = lax.axis_size("clip")
    shards = lax.axis_size("cap")
    devices = clip_devices * shards
    clips, frame_max, patch_rows, width = patches.shape
    text_rows = text.shape[0]
    own_rows = text_rows // devices
    scale = width ** (-0.5)
    flat_rows = clips * patch_rows * frame_max
    assert WORDS % own_rows == 0 and WORDS % clips == 0
    limit = pltpu.CompilerParams(vmem_limit_bytes=24 << 20)

    flat = patches.transpose(0, 2, 1, 3).reshape(flat_rows, width)
    stats, scores, flat_near, text_near = pl.pallas_call(
        functools.partial(forward_kernel, clips, frame_max, scale),
        out_shape=(
            jax.ShapeDtypeStruct((3 * clips, text_rows), F32),
            pltpu.VMEM((flat_rows, text_rows), F32),
            pltpu.VMEM((flat_rows, width), BF16),
            pltpu.VMEM((text_rows, width), BF16),
        ),
        in_specs=[ANY, ANY, ANY],
        out_specs=(VMEM, VMEM, VMEM, VMEM),
        scratch_shapes=[
            pltpu.SMEM(frame_slots.shape, jnp.int32),
            pltpu.SemaphoreType.DMA((clips * FORWARD_PARTS + 2,)),
        ],
        compiler_params=limit,
        name="forward",
    )(far(text), far(flat), far(frame_slots))
    parts = [stats] + exchange(stats, "cap")
    sent, slopes = pl.pallas_call(
        functools.partial(middle_kernel, clips, frame_max, shards, scale),
        out_shape=(
            jax.ShapeDtypeStruct((devices, own_rows, clips * width + text_rows), BF16),
            pltpu.VMEM((flat_rows, text_rows), F32),
        ),
        in_specs=[VMEM] * (shards + 2),
        out_specs=(VMEM, VMEM),
        compiler_params=limit,
        name="middle",
    )(*parts, scores, flat_near)
    got = lax.all_to_all(sent, AXES, split_axis=0, concat_axis=0, tiled=True)
    loss, flat_grad, text_grad = pl.pallas_call(
        functools.partial(backward_kernel, clips, frame_max, shards, scale),
        out_shape=(
            pltpu.HBM((1, 1), F32),
            pltpu.HBM((flat_rows, width), BF16),
            pltpu.HBM((own_rows, width), F32),
        ),
        in_specs=[VMEM, VMEM, VMEM],
        out_specs=(ANY, ANY, ANY),
        scratch_shapes=[
            pltpu.VMEM((flat_rows, width), BF16),
            pltpu.VMEM((1, 1), F32),
            pltpu.VMEM((own_rows, width), F32),
            pltpu.SemaphoreType.DMA((clips * BACKWARD_PARTS + 2,)),
        ],
        compiler_params=limit,
        name="backward",
    )(got, slopes, text_near)
    patch_grad = flat_grad.reshape(clips, patch_rows, frame_max, width).transpose(0, 2, 1, 3)
    return (loss[0, 0], patch_grad, text_grad)


def solution(mesh):
    return jax.shard_map(
        per_device,
        mesh=mesh,
        in_specs=(P(), P("clip", None, "cap", None), P("clip", None)),
        out_specs=(P(), P("clip", None, "cap", None), P(AXES, None)),
        check_vma=False,
    )
```

```python
import functools

import jax
import jax.numpy as jnp
from jax import lax
from jax.experimental import pallas as pl
from jax.experimental.pallas import tpu as pltpu
from jax.sharding import PartitionSpec as P

WORDS = 8
AXES = ("clip", "cap")

logit_scale = 32.0
loss_scale = 8192.0
big_value = 1e30

F32 = jnp.float32
BF16 = jnp.bfloat16
ANY = pl.BlockSpec(memory_space=pl.ANY)
VMEM = pl.BlockSpec(memory_space=pltpu.VMEM)


BACKWARD_PARTS = 2
SCORE_PARTS = 2


def row_parts(columns, frame_max, parts):
    patch_rows = columns // frame_max
    edges = [patch_rows * k // parts * frame_max for k in range(parts + 1)]
    return [(a, b - a) for a, b in zip(edges, edges[1:])]


def valid_mask(slots_ref, v, frame_max, lanes):
    count = jnp.int32(0)
    for f in range(frame_max):
        count += (slots_ref[v, f] >= 0).astype(jnp.int32)
    return lax.broadcasted_iota(jnp.int32, (1, frame_max, lanes), 1) < count


def own_half(rows, own_rows):
    split = rows.reshape(-1, 2, own_rows, rows.shape[-1])
    even_rows = split[:, 0].reshape(-1, rows.shape[-1])
    odd_rows = split[:, 1].reshape(-1, rows.shape[-1])
    odd = (lax.axis_index("cap") & 1) == 1
    return jnp.where(odd, odd_rows, even_rows), jnp.where(odd, even_rows, odd_rows)


def forward_kernel(
    clips, frame_max, own_rows, scale,
    text_hbm, flat_hbm, slots_hbm,
    stats_ref, scores_ref, text_ref, give_ref, keep_ref,
    flat_ref, slots_ref, sems,
):
    columns, width = flat_ref.shape[0] // clips, flat_ref.shape[1]
    lanes = text_ref.shape[0]
    runs = [pl.ds(v * columns, columns) for v in range(clips)]
    copies = [
        pltpu.make_async_copy(flat_hbm.at[run], flat_ref.at[run], sems.at[v])
        for v, run in enumerate(runs)
    ]
    text_copy = pltpu.make_async_copy(text_hbm, text_ref, sems.at[clips])
    slots_copy = pltpu.make_async_copy(slots_hbm, slots_ref, sems.at[clips + 1])
    text_copy.start()
    slots_copy.start()
    for copy in copies:
        copy.start()
    slots_copy.wait()
    masks = [valid_mask(slots_ref, v, frame_max, lanes) for v in range(clips)]
    text_copy.wait()

    def score(v):
        peak = jnp.full((frame_max, lanes), -big_value, F32)
        for start, size in row_parts(columns, frame_max, SCORE_PARTS):
            run = pl.ds(v * columns + start, size)
            part = lax.dot_general(
                flat_ref[run], text_ref[...], (((1,), (1,)), ((), ())), preferred_element_type=F32
            ) * scale
            part = jnp.where(masks[v], part.reshape(-1, frame_max, lanes), -big_value)
            scores_ref[run] = part.reshape(-1, lanes)
            peak = jnp.maximum(peak, jnp.max(part, axis=0))
        return jnp.max(peak, axis=0, keepdims=True)

    def pool(v, peak):
        part = scores_ref[runs[v]].reshape(-1, frame_max, lanes)
        weight = jnp.exp(part - peak[None])
        total = jnp.sum(jnp.sum(weight, axis=0), axis=0, keepdims=True)
        weighted = jnp.sum(jnp.sum(weight * part, axis=0), axis=0, keepdims=True)
        stats_ref[pl.ds(v, 1)] = peak
        stats_ref[pl.ds(clips + v, 1)] = total
        stats_ref[pl.ds(2 * clips + v, 1)] = weighted
        slope = weight * (1.0 + part - (weighted / total)[None])
        both = jnp.concatenate(
            [slope.reshape(columns, lanes).astype(BF16), weight.reshape(columns, lanes).astype(BF16)],
            axis=1,
        )
        grads = lax.dot_general(
            both, flat_ref[runs[v]], (((0,), (0,)), ((), ())), preferred_element_type=F32
        ) * scale
        for q in range(2):
            keep, give = own_half(grads[q * lanes : (q + 1) * lanes], own_rows)
            span = pl.ds((2 * v + q) * width, width)
            keep_ref[:, span] = keep
            give_ref[:, span] = give

    peaks = []
    for v in range(clips):
        copies[v].wait()
        peaks.append(score(v))
    for v in range(clips):
        pool(v, peaks[v])


def caption_mean(row, lanes):
    row = jnp.broadcast_to(row, (8, lanes))
    lane = lax.broadcasted_iota(jnp.int32, (8, lanes), 1)
    step = 1
    while step < WORDS:
        up = pltpu.roll(row, lanes - step, 1)
        down = pltpu.roll(row, step, 1)
        row = row + jnp.where((lane & step) == 0, up, down)
        step *= 2
    return row * (1.0 / WORDS)


def merge(clips, stats, v):
    peaks = [s[pl.ds(v, 1)] for s in stats]
    totals = [s[pl.ds(clips + v, 1)] for s in stats]
    weighted = [s[pl.ds(2 * clips + v, 1)] for s in stats]
    peak = functools.reduce(jnp.maximum, peaks)
    factors = [jnp.exp(p - peak) for p in peaks]
    inverse = 1.0 / sum(f * t for f, t in zip(factors, totals))
    pooled = sum(f * w for f, w in zip(factors, weighted)) * inverse
    shares = [(f * inverse, w / t - pooled) for f, w, t in zip(factors, weighted, totals)]
    return peak, inverse, pooled, shares


def pack_kernel(clips, shards, *refs):
    stats = refs[:shards]
    keep_ref, got_ref, send_ref = refs[shards:]
    pairs, own_rows, _ = send_ref.shape
    width = keep_ref.shape[1] // (2 * clips)
    lanes = stats[0].shape[1]
    group = WORDS // clips
    lane = lax.broadcasted_iota(jnp.int32, (8, lanes), 1)
    means = None
    columns = []
    for v in range(clips):
        _, _, pooled, shares = merge(clips, stats, v)
        mean = caption_mean(pooled, lanes)
        inside = (lane & (WORDS - 1)) >= v * group
        means = mean if means is None else jnp.where(inside, mean, means)
        for factor, shift in shares[:2]:
            columns += [factor, factor * shift]
    fill = -len(columns) % 8
    columns += [jnp.zeros((1, lanes), F32)] * fill
    columns, _ = own_half(jnp.concatenate(columns, axis=0).T, own_rows)
    for v in range(clips):
        out = None
        for n, ref in enumerate((keep_ref, got_ref)):
            for q in range(2):
                k = 4 * v + 2 * n + q
                term = columns[:, k : k + 1] * ref[:, pl.ds((2 * v + q) * width, width)]
                out = term if out is None else out + term
        send_ref[:, :, pl.ds(v * width, width)] = out.reshape(pairs, own_rows, width).astype(BF16)
    high = means.astype(BF16)
    rest = means - high.astype(F32)
    middle = rest.astype(BF16)
    low = (rest - middle.astype(F32)).astype(BF16)
    row = lax.broadcasted_iota(jnp.int32, (own_rows, lanes), 0)
    pieces = [p.astype(F32)[:1] for p in (high, middle, low)]
    block = jnp.where(row == 0, pieces[0], jnp.where(row == 1, pieces[1], jnp.where(row == 2, pieces[2], 0.0)))
    send_ref[:, :, pl.ds(clips * width, lanes)] = jnp.broadcast_to(
        block.astype(BF16)[None], (pairs, own_rows, lanes)
    )


def backward_kernel(
    clips, frame_max, shards, scale,
    got_ref, scores_ref, text_ref, *refs,
):
    stats = refs[:shards]
    loss_hbm, flat_grad_hbm, text_grad_hbm, staged_ref, loss_ref, text_grad_ref, sems = refs[shards:]
    lanes, width = text_ref.shape
    senders, own_rows, _ = got_ref.shape
    owners = lax.axis_size("clip")
    shares = senders // owners
    clip_total = owners * clips
    captions = lanes // WORDS
    group = WORDS // clips
    rank = lax.axis_index("clip")
    device = rank * shards + lax.axis_index("cap")
    lane = lax.broadcasted_iota(jnp.int32, (1, lanes), 1)
    word = lane & (WORDS - 1)
    rows = []
    for i in range(owners):
        pieces = got_ref[i * shares, :, pl.ds(clips * width, lanes)].astype(F32)
        rows.append(pieces[0:1] + pieces[1:2] + pieces[2:3])
    packed = jnp.concatenate(rows, axis=0)
    by_clip = []
    for v in range(clips):
        mean = packed
        step = group
        while step < WORDS:
            up = pltpu.roll(mean, lanes - step, 1)
            down = pltpu.roll(mean, step, 1)
            keep = ((word & step) != 0) == ((v * group & step) != 0)
            mean = jnp.where(keep, mean, jnp.where((word & step) == 0, up, down))
            step *= 2
        by_clip.append(logit_scale * mean)
    owner = lax.broadcasted_iota(jnp.int32, (owners, lanes), 0)
    caption = lax.broadcasted_iota(jnp.int32, (owners, lanes), 1) // WORDS
    row_max = functools.reduce(jnp.maximum, [jnp.max(b, axis=0, keepdims=True) for b in by_clip])
    row_exp = [jnp.exp(b - row_max) for b in by_clip]
    row_sum = sum(jnp.sum(e, axis=0, keepdims=True) for e in row_exp)
    per_word = 1.0 / WORDS
    loss = jnp.sum(row_max + jnp.log(row_sum), axis=1, keepdims=True) * per_word
    factor = logit_scale / WORDS * loss_scale * 0.5 / clip_total
    grads = []
    for v in range(clips):
        col_max = jnp.max(by_clip[v], axis=1, keepdims=True)
        col_exp = jnp.exp(by_clip[v] - col_max)
        col_sum = jnp.sum(col_exp, axis=1, keepdims=True) * per_word
        same = caption == owner * clips + v
        loss += jnp.sum(col_max + jnp.log(col_sum), axis=0, keepdims=True)
        matched = jnp.where(same, by_clip[v], 0.0)
        loss -= 2.0 * per_word * jnp.sum(jnp.sum(matched, axis=1, keepdims=True), axis=0, keepdims=True)
        grads.append(
            factor * (row_exp[v] / row_sum + col_exp / col_sum - jnp.where(same, 2.0, 0.0))
        )
    loss_ref[...] = loss * (0.5 / clip_total)
    copies = [pltpu.make_async_copy(loss_ref, loss_hbm, sems.at[0])]
    copies[0].start()

    columns = scores_ref.shape[0] // clips
    parts = row_parts(columns, frame_max, BACKWARD_PARTS)
    for v in range(clips):
        mine = jnp.sum(jnp.where(owner == rank, grads[v], 0.0), axis=0, keepdims=True)
        peak, inverse, pooled, _ = merge(clips, stats, v)
        mine = mine * inverse
        for start, size in parts:
            run = pl.ds(v * columns + start, size)
            part = scores_ref[run]
            grad_scores = (mine * jnp.exp(part - peak) * (1.0 + part - pooled)).astype(BF16)
            staged_ref[run] = (
                jnp.dot(grad_scores, text_ref[...], preferred_element_type=F32) * scale
            ).astype(BF16)
            copy = pltpu.make_async_copy(
                staged_ref.at[run], flat_grad_hbm.at[run], sems.at[len(copies)]
            )
            copy.start()
            copies.append(copy)
    chosen = lax.broadcasted_iota(jnp.int32, (owners, lanes), 1) == device * own_rows
    out = jnp.zeros((own_rows, width), F32)
    for v in range(clips):
        column = jnp.sum(jnp.where(chosen, grads[v], 0.0), axis=1, keepdims=True)
        for i in range(owners):
            part = jnp.zeros((own_rows, width), F32)
            for k in range(shares):
                part += got_ref[i * shares + k, :, pl.ds(v * width, width)].astype(F32)
            out += column[i : i + 1, :] * part
    text_grad_ref[...] = out
    copies.append(pltpu.make_async_copy(text_grad_ref, text_grad_hbm, sems.at[len(copies)]))
    copies[-1].start()
    for copy in copies:
        copy.wait()


def exchange(value, axis):
    size = lax.axis_size(axis)
    got = []
    for k in range(1, size):
        if size & (size - 1) == 0:
            pairs = [(i, i ^ k) for i in range(size)]
        else:
            pairs = [(i, (i + k) % size) for i in range(size)]
        got.append(lax.ppermute(value, axis, pairs))
    return got


def far(x):
    return pltpu.with_memory_space_constraint(x, pltpu.HBM)


def per_device(text, patches, frame_slots):
    clip_devices = lax.axis_size("clip")
    shards = lax.axis_size("cap")
    devices = clip_devices * shards
    clips, frame_max, patch_rows, width = patches.shape
    text_rows = text.shape[0]
    own_rows = text_rows // devices
    scale = width ** (-0.5)
    flat_rows = clips * patch_rows * frame_max
    pairs = devices // 2
    assert WORDS % own_rows == 0 and WORDS % clips == 0 and shards & (shards - 1) == 0
    assert shards > 1
    limit = pltpu.CompilerParams(vmem_limit_bytes=24 << 20)

    flat = patches.transpose(0, 2, 1, 3).reshape(flat_rows, width)
    stats, scores, text_near, give, keep = pl.pallas_call(
        functools.partial(forward_kernel, clips, frame_max, own_rows, scale),
        out_shape=(
            pltpu.VMEM((3 * clips, text_rows), F32),
            pltpu.VMEM((flat_rows, text_rows), F32),
            pltpu.VMEM((text_rows, width), BF16),
            pltpu.VMEM((text_rows // 2, 2 * clips * width), F32),
            pltpu.VMEM((text_rows // 2, 2 * clips * width), F32),
        ),
        in_specs=[ANY] * 3,
        out_specs=(VMEM,) * 5,
        scratch_shapes=[
            pltpu.VMEM((flat_rows, width), BF16),
            pltpu.SMEM(frame_slots.shape, jnp.int32),
            pltpu.SemaphoreType.DMA((clips + 2,)),
        ],
        compiler_params=limit,
        name="forward",
    )(far(text), far(flat), far(frame_slots))
    got = lax.ppermute(give, AXES, [(d, d ^ 1) for d in range(devices)])
    shares = [stats] + exchange(stats, "cap")
    sent = pl.pallas_call(
        functools.partial(pack_kernel, clips, shards),
        out_shape=pltpu.VMEM((pairs, own_rows, clips * width + text_rows), BF16),
        in_specs=[VMEM] * (shards + 2),
        out_specs=VMEM,
        compiler_params=limit,
        name="pack",
    )(*shares, keep, got)
    halves = [[2 * k + side for k in range(pairs)] for side in range(2)]
    got = lax.all_to_all(
        sent, AXES, split_axis=0, concat_axis=0, tiled=True, axis_index_groups=halves
    )
    loss, flat_grad, text_grad = pl.pallas_call(
        functools.partial(backward_kernel, clips, frame_max, shards, scale),
        out_shape=(
            pltpu.HBM((1, 1), F32),
            pltpu.HBM((flat_rows, width), BF16),
            pltpu.HBM((own_rows, width), F32),
        ),
        in_specs=[VMEM] * (shards + 3),
        out_specs=(ANY, ANY, ANY),
        scratch_shapes=[
            pltpu.VMEM((flat_rows, width), BF16),
            pltpu.VMEM((1, 1), F32),
            pltpu.VMEM((own_rows, width), F32),
            pltpu.SemaphoreType.DMA((clips * BACKWARD_PARTS + 2,)),
        ],
        compiler_params=limit,
        name="backward",
    )(got, scores, text_near, *shares)
    patch_grad = flat_grad.reshape(clips, patch_rows, frame_max, width).transpose(0, 2, 1, 3)
    return (loss[0, 0], patch_grad, text_grad)


def solution(mesh):
    return jax.shard_map(
        per_device,
        mesh=mesh,
        in_specs=(P(), P("clip", None, "cap", None), P("clip", None)),
        out_specs=(P(), P("clip", None, "cap", None), P(AXES, None)),
        check_vma=False,
    )
```

```python
import functools

import jax
import jax.numpy as jnp
from jax import lax
from jax.experimental import pallas as pl
from jax.experimental.pallas import tpu as pltpu
from jax.sharding import PartitionSpec as P

WORDS = 8
AXES = ("clip", "cap")

logit_scale = 32.0
loss_scale = 8192.0
big_value = 1e30

F32 = jnp.float32
BF16 = jnp.bfloat16
ANY = pl.BlockSpec(memory_space=pl.ANY)
VMEM = pl.BlockSpec(memory_space=pltpu.VMEM)


BACKWARD_PARTS = 2
SCORE_PARTS = 2


def row_parts(columns, frame_max, parts):
    patch_rows = columns // frame_max
    edges = [patch_rows * k // parts * frame_max for k in range(parts + 1)]
    return [(a, b - a) for a, b in zip(edges, edges[1:])]


def valid_mask(slots_ref, v, frame_max, lanes):
    count = jnp.int32(0)
    for f in range(frame_max):
        count += (slots_ref[v, f] >= 0).astype(jnp.int32)
    return lax.broadcasted_iota(jnp.int32, (1, frame_max, lanes), 1) < count


def own_half(rows, own_rows):
    split = rows.reshape(-1, 2, own_rows, rows.shape[-1])
    even_rows = split[:, 0].reshape(-1, rows.shape[-1])
    odd_rows = split[:, 1].reshape(-1, rows.shape[-1])
    odd = (lax.axis_index("cap") & 1) == 1
    return jnp.where(odd, odd_rows, even_rows), jnp.where(odd, even_rows, odd_rows)


def forward_kernel(
    clips, frame_max, own_rows, scale,
    text_hbm, flat_hbm, slots_hbm,
    stats_ref, scores_ref, text_ref, give_ref, keep_ref,
    flat_ref, slots_ref, sems,
):
    columns, width = flat_ref.shape[0] // clips, flat_ref.shape[1]
    lanes = text_ref.shape[0]
    runs = [pl.ds(v * columns, columns) for v in range(clips)]
    copies = [
        pltpu.make_async_copy(flat_hbm.at[run], flat_ref.at[run], sems.at[v])
        for v, run in enumerate(runs)
    ]
    text_copy = pltpu.make_async_copy(text_hbm, text_ref, sems.at[clips])
    slots_copy = pltpu.make_async_copy(slots_hbm, slots_ref, sems.at[clips + 1])
    text_copy.start()
    slots_copy.start()
    for copy in copies:
        copy.start()
    slots_copy.wait()
    masks = [valid_mask(slots_ref, v, frame_max, lanes) for v in range(clips)]
    text_copy.wait()

    def score(v):
        peak = jnp.full((frame_max, lanes), -big_value, F32)
        for start, size in row_parts(columns, frame_max, SCORE_PARTS):
            run = pl.ds(v * columns + start, size)
            part = lax.dot_general(
                flat_ref[run], text_ref[...], (((1,), (1,)), ((), ())), preferred_element_type=F32
            ) * scale
            part = jnp.where(masks[v], part.reshape(-1, frame_max, lanes), -big_value)
            scores_ref[run] = part.reshape(-1, lanes)
            peak = jnp.maximum(peak, jnp.max(part, axis=0))
        return jnp.max(peak, axis=0, keepdims=True)

    def pool(v, peak):
        part = scores_ref[runs[v]].reshape(-1, frame_max, lanes)
        weight = jnp.exp(part - peak[None])
        total = jnp.sum(jnp.sum(weight, axis=0), axis=0, keepdims=True)
        weighted = jnp.sum(jnp.sum(weight * part, axis=0), axis=0, keepdims=True)
        stats_ref[pl.ds(v, 1)] = peak
        stats_ref[pl.ds(clips + v, 1)] = total
        stats_ref[pl.ds(2 * clips + v, 1)] = weighted
        slope = weight * (1.0 + part - (weighted / total)[None])
        both = jnp.concatenate(
            [slope.reshape(columns, lanes).astype(BF16), weight.reshape(columns, lanes).astype(BF16)],
            axis=1,
        )
        grads = lax.dot_general(
            both, flat_ref[runs[v]], (((0,), (0,)), ((), ())), preferred_element_type=F32
        ) * scale
        for q in range(2):
            keep, give = own_half(grads[q * lanes : (q + 1) * lanes], own_rows)
            span = pl.ds((2 * v + q) * width, width)
            keep_ref[:, span] = keep
            give_ref[:, span] = give

    peaks = []
    for v in range(clips):
        copies[v].wait()
        peaks.append(score(v))
    for v in range(clips):
        pool(v, peaks[v])


def caption_mean(row, lanes):
    row = jnp.broadcast_to(row, (8, lanes))
    lane = lax.broadcasted_iota(jnp.int32, (8, lanes), 1)
    step = 1
    while step < WORDS:
        up = pltpu.roll(row, lanes - step, 1)
        down = pltpu.roll(row, step, 1)
        row = row + jnp.where((lane & step) == 0, up, down)
        step *= 2
    return row * (1.0 / WORDS)


def merge(clips, stats, v):
    peaks = [s[pl.ds(v, 1)] for s in stats]
    totals = [s[pl.ds(clips + v, 1)] for s in stats]
    weighted = [s[pl.ds(2 * clips + v, 1)] for s in stats]
    peak = functools.reduce(jnp.maximum, peaks)
    factors = [jnp.exp(p - peak) for p in peaks]
    inverse = 1.0 / sum(f * t for f, t in zip(factors, totals))
    pooled = sum(f * w for f, w in zip(factors, weighted)) * inverse
    shares = [(f * inverse, w / t - pooled) for f, w, t in zip(factors, weighted, totals)]
    return peak, inverse, pooled, shares


def pair_slots(pairs):
    return [(pair + 1) % pairs for pair in range(pairs)]


def pack_kernel(clips, shards, *refs):
    stats = refs[:shards]
    keep_ref, got_ref, send_ref = refs[shards:]
    pairs, own_rows, _ = send_ref.shape
    width = keep_ref.shape[1] // (2 * clips)
    lanes = stats[0].shape[1]
    group = WORDS // clips
    lane = lax.broadcasted_iota(jnp.int32, (8, lanes), 1)
    means = None
    columns = []
    for v in range(clips):
        _, _, pooled, shares = merge(clips, stats, v)
        mean = caption_mean(pooled, lanes)
        inside = (lane & (WORDS - 1)) >= v * group
        means = mean if means is None else jnp.where(inside, mean, means)
        for factor, shift in shares[:2]:
            columns += [factor, factor * shift]
    fill = -len(columns) % 8
    columns += [jnp.zeros((1, lanes), F32)] * fill
    columns, _ = own_half(jnp.concatenate(columns, axis=0).T, own_rows)
    for v in range(clips):
        out = None
        for n, ref in enumerate((keep_ref, got_ref)):
            for q in range(2):
                k = 4 * v + 2 * n + q
                term = columns[:, k : k + 1] * ref[:, pl.ds((2 * v + q) * width, width)]
                out = term if out is None else out + term
        out = out.reshape(pairs, own_rows, width).astype(BF16)
        for pair, slot in enumerate(pair_slots(pairs)):
            send_ref[slot, :, pl.ds(v * width, width)] = out[pair]
    high = means.astype(BF16)
    rest = means - high.astype(F32)
    middle = rest.astype(BF16)
    low = (rest - middle.astype(F32)).astype(BF16)
    row = lax.broadcasted_iota(jnp.int32, (own_rows, lanes), 0)
    pieces = [p.astype(F32)[:1] for p in (high, middle, low)]
    block = jnp.where(row == 0, pieces[0], jnp.where(row == 1, pieces[1], jnp.where(row == 2, pieces[2], 0.0)))
    send_ref[:, :, pl.ds(clips * width, lanes)] = jnp.broadcast_to(
        block.astype(BF16)[None], (pairs, own_rows, lanes)
    )


def backward_kernel(
    clips, frame_max, shards, scale,
    got_ref, scores_ref, text_ref, *refs,
):
    stats = refs[:shards]
    loss_hbm, flat_grad_hbm, text_grad_hbm, staged_ref, loss_ref, text_grad_ref, sems = refs[shards:]
    lanes, width = text_ref.shape
    senders, own_rows, _ = got_ref.shape
    owners = lax.axis_size("clip")
    shares = senders // owners
    slots = pair_slots(senders)
    clip_total = owners * clips
    group = WORDS // clips
    rank = lax.axis_index("clip")
    device = rank * shards + lax.axis_index("cap")
    lane = lax.broadcasted_iota(jnp.int32, (1, lanes), 1)
    word = lane & (WORDS - 1)
    rows = []
    for i in range(owners):
        pieces = got_ref[slots[i * shares], :, pl.ds(clips * width, lanes)].astype(F32)
        rows.append(pieces[0:1] + pieces[1:2] + pieces[2:3])
    packed = jnp.concatenate(rows, axis=0)
    by_clip = []
    for v in range(clips):
        mean = packed
        step = group
        while step < WORDS:
            up = pltpu.roll(mean, lanes - step, 1)
            down = pltpu.roll(mean, step, 1)
            keep = ((word & step) != 0) == ((v * group & step) != 0)
            mean = jnp.where(keep, mean, jnp.where((word & step) == 0, up, down))
            step *= 2
        by_clip.append(logit_scale * mean)
    owner = lax.broadcasted_iota(jnp.int32, (owners, lanes), 0)
    caption = lax.broadcasted_iota(jnp.int32, (owners, lanes), 1) // WORDS
    row_max = functools.reduce(jnp.maximum, [jnp.max(b, axis=0, keepdims=True) for b in by_clip])
    row_exp = [jnp.exp(b - row_max) for b in by_clip]
    row_sum = sum(jnp.sum(e, axis=0, keepdims=True) for e in row_exp)
    per_word = 1.0 / WORDS
    loss = jnp.sum(row_max + jnp.log(row_sum), axis=1, keepdims=True) * per_word
    factor = logit_scale / WORDS * loss_scale * 0.5 / clip_total
    grads = []
    for v in range(clips):
        col_max = jnp.max(by_clip[v], axis=1, keepdims=True)
        col_exp = jnp.exp(by_clip[v] - col_max)
        col_sum = jnp.sum(col_exp, axis=1, keepdims=True) * per_word
        same = caption == owner * clips + v
        loss += jnp.sum(col_max + jnp.log(col_sum), axis=0, keepdims=True)
        matched = jnp.where(same, by_clip[v], 0.0)
        loss -= 2.0 * per_word * jnp.sum(jnp.sum(matched, axis=1, keepdims=True), axis=0, keepdims=True)
        grads.append(
            factor * (row_exp[v] / row_sum + col_exp / col_sum - jnp.where(same, 2.0, 0.0))
        )
    loss_ref[...] = loss * (0.5 / clip_total)
    copies = [pltpu.make_async_copy(loss_ref, loss_hbm, sems.at[0])]
    copies[0].start()

    columns = scores_ref.shape[0] // clips
    parts = row_parts(columns, frame_max, BACKWARD_PARTS)
    for v in range(clips):
        mine = jnp.sum(jnp.where(owner == rank, grads[v], 0.0), axis=0, keepdims=True)
        peak, inverse, pooled, _ = merge(clips, stats, v)
        mine = mine * inverse
        for start, size in parts:
            run = pl.ds(v * columns + start, size)
            part = scores_ref[run]
            grad_scores = (mine * jnp.exp(part - peak) * (1.0 + part - pooled)).astype(BF16)
            staged_ref[run] = (
                jnp.dot(grad_scores, text_ref[...], preferred_element_type=F32) * scale
            ).astype(BF16)
            copy = pltpu.make_async_copy(
                staged_ref.at[run], flat_grad_hbm.at[run], sems.at[len(copies)]
            )
            copy.start()
            copies.append(copy)
    chosen = lax.broadcasted_iota(jnp.int32, (owners, lanes), 1) == device * own_rows
    out = jnp.zeros((own_rows, width), F32)
    for v in range(clips):
        column = jnp.sum(jnp.where(chosen, grads[v], 0.0), axis=1, keepdims=True)
        for i in range(owners):
            part = jnp.zeros((own_rows, width), F32)
            for k in range(shares):
                part += got_ref[slots[i * shares + k], :, pl.ds(v * width, width)].astype(F32)
            out += column[i : i + 1, :] * part
    text_grad_ref[...] = out
    copies.append(pltpu.make_async_copy(text_grad_ref, text_grad_hbm, sems.at[len(copies)]))
    copies[-1].start()
    for copy in copies:
        copy.wait()


def exchange(value, axis):
    size = lax.axis_size(axis)
    got = []
    for k in range(1, size):
        if size & (size - 1) == 0:
            pairs = [(i, i ^ k) for i in range(size)]
        else:
            pairs = [(i, (i + k) % size) for i in range(size)]
        got.append(lax.ppermute(value, axis, pairs))
    return got


def far(x):
    return pltpu.with_memory_space_constraint(x, pltpu.HBM)


def per_device(text, patches, frame_slots):
    clip_devices = lax.axis_size("clip")
    shards = lax.axis_size("cap")
    devices = clip_devices * shards
    clips, frame_max, patch_rows, width = patches.shape
    text_rows = text.shape[0]
    own_rows = text_rows // devices
    scale = width ** (-0.5)
    flat_rows = clips * patch_rows * frame_max
    pairs = devices // 2
    assert WORDS % own_rows == 0 and WORDS % clips == 0 and shards & (shards - 1) == 0
    assert shards > 1
    limit = pltpu.CompilerParams(vmem_limit_bytes=24 << 20)

    flat = patches.transpose(0, 2, 1, 3).reshape(flat_rows, width)
    stats, scores, text_near, give, keep = pl.pallas_call(
        functools.partial(forward_kernel, clips, frame_max, own_rows, scale),
        out_shape=(
            pltpu.VMEM((3 * clips, text_rows), F32),
            pltpu.VMEM((flat_rows, text_rows), F32),
            pltpu.VMEM((text_rows, width), BF16),
            pltpu.VMEM((text_rows // 2, 2 * clips * width), F32),
            pltpu.VMEM((text_rows // 2, 2 * clips * width), F32),
        ),
        in_specs=[ANY] * 3,
        out_specs=(VMEM,) * 5,
        scratch_shapes=[
            pltpu.VMEM((flat_rows, width), BF16),
            pltpu.SMEM(frame_slots.shape, jnp.int32),
            pltpu.SemaphoreType.DMA((clips + 2,)),
        ],
        compiler_params=limit,
        name="forward",
    )(far(text), far(flat), far(frame_slots))
    got = lax.ppermute(give, AXES, [(d, d ^ 1) for d in range(devices)])
    shares = [stats] + exchange(stats, "cap")
    sent = pl.pallas_call(
        functools.partial(pack_kernel, clips, shards),
        out_shape=pltpu.VMEM((pairs, own_rows, clips * width + text_rows), BF16),
        in_specs=[VMEM] * (shards + 2),
        out_specs=VMEM,
        compiler_params=limit,
        name="pack",
    )(*shares, keep, got)
    slots = pair_slots(pairs)
    halves = [[2 * slots.index(k) + side for k in range(pairs)] for side in range(2)]
    got = lax.all_to_all(
        sent, AXES, split_axis=0, concat_axis=0, tiled=True, axis_index_groups=halves
    )
    loss, flat_grad, text_grad = pl.pallas_call(
        functools.partial(backward_kernel, clips, frame_max, shards, scale),
        out_shape=(
            pltpu.HBM((1, 1), F32),
            pltpu.HBM((flat_rows, width), BF16),
            pltpu.HBM((own_rows, width), F32),
        ),
        in_specs=[VMEM] * (shards + 3),
        out_specs=(ANY, ANY, ANY),
        scratch_shapes=[
            pltpu.VMEM((flat_rows, width), BF16),
            pltpu.VMEM((1, 1), F32),
            pltpu.VMEM((own_rows, width), F32),
            pltpu.SemaphoreType.DMA((clips * BACKWARD_PARTS + 2,)),
        ],
        compiler_params=limit,
        name="backward",
    )(got, scores, text_near, *shares)
    patch_grad = flat_grad.reshape(clips, patch_rows, frame_max, width).transpose(0, 2, 1, 3)
    return (loss[0, 0], patch_grad, text_grad)


def solution(mesh):
    return jax.shard_map(
        per_device,
        mesh=mesh,
        in_specs=(P(), P("clip", None, "cap", None), P("clip", None)),
        out_specs=(P(), P("clip", None, "cap", None), P(AXES, None)),
        check_vma=False,
    )
```

```python
import functools

import jax
import jax.numpy as jnp
from jax import lax
from jax.experimental import pallas as pl
from jax.experimental.pallas import tpu as pltpu
from jax.sharding import PartitionSpec as P

WORDS = 8
AXES = ("clip", "cap")

logit_scale = 32.0
loss_scale = 8192.0
big_value = 1e30

F32 = jnp.float32
BF16 = jnp.bfloat16
ANY = pl.BlockSpec(memory_space=pl.ANY)
VMEM = pl.BlockSpec(memory_space=pltpu.VMEM)


BACKWARD_PARTS = 2
SCORE_PARTS = 2


def row_parts(columns, frame_max, parts):
    patch_rows = columns // frame_max
    edges = [patch_rows * k // parts * frame_max for k in range(parts + 1)]
    return [(a, b - a) for a, b in zip(edges, edges[1:])]


def valid_mask(slots_ref, v, frame_max, lanes):
    count = jnp.int32(0)
    for f in range(frame_max):
        count += (slots_ref[v, f] >= 0).astype(jnp.int32)
    return lax.broadcasted_iota(jnp.int32, (1, frame_max, lanes), 1) < count


def own_half(rows, own_rows):
    split = rows.reshape(-1, 2, own_rows, rows.shape[-1])
    even_rows = split[:, 0].reshape(-1, rows.shape[-1])
    odd_rows = split[:, 1].reshape(-1, rows.shape[-1])
    odd = (lax.axis_index("cap") & 1) == 1
    return jnp.where(odd, odd_rows, even_rows), jnp.where(odd, even_rows, odd_rows)


def forward_kernel(
    clips, frame_max, own_rows, scale,
    text_hbm, flat_hbm, slots_hbm,
    stats_ref, scores_ref, text_ref, give_ref, keep_ref,
    flat_ref, slots_ref, sems,
):
    columns, width = flat_ref.shape[0] // clips, flat_ref.shape[1]
    lanes = text_ref.shape[0]
    runs = [pl.ds(v * columns, columns) for v in range(clips)]
    copies = [
        pltpu.make_async_copy(flat_hbm.at[run], flat_ref.at[run], sems.at[v])
        for v, run in enumerate(runs)
    ]
    text_copy = pltpu.make_async_copy(text_hbm, text_ref, sems.at[clips])
    slots_copy = pltpu.make_async_copy(slots_hbm, slots_ref, sems.at[clips + 1])
    text_copy.start()
    slots_copy.start()
    for copy in copies:
        copy.start()
    slots_copy.wait()
    masks = [valid_mask(slots_ref, v, frame_max, lanes) for v in range(clips)]
    text_copy.wait()

    def score(v):
        peak = jnp.full((frame_max, lanes), -big_value, F32)
        for start, size in row_parts(columns, frame_max, SCORE_PARTS):
            run = pl.ds(v * columns + start, size)
            part = lax.dot_general(
                flat_ref[run], text_ref[...], (((1,), (1,)), ((), ())), preferred_element_type=F32
            ) * scale
            part = jnp.where(masks[v], part.reshape(-1, frame_max, lanes), -big_value)
            scores_ref[run] = part.reshape(-1, lanes)
            peak = jnp.maximum(peak, jnp.max(part, axis=0))
        return jnp.max(peak, axis=0, keepdims=True)

    def pool(v, peak):
        part = scores_ref[runs[v]].reshape(-1, frame_max, lanes)
        weight = jnp.exp(part - peak[None])
        total = jnp.sum(jnp.sum(weight, axis=0), axis=0, keepdims=True)
        weighted = jnp.sum(jnp.sum(weight * part, axis=0), axis=0, keepdims=True)
        stats_ref[pl.ds(v, 1)] = peak
        stats_ref[pl.ds(clips + v, 1)] = total
        stats_ref[pl.ds(2 * clips + v, 1)] = weighted
        slope = weight * (1.0 + part - (weighted / total)[None])
        both = jnp.concatenate(
            [slope.reshape(columns, lanes).astype(BF16), weight.reshape(columns, lanes).astype(BF16)],
            axis=1,
        )
        grads = lax.dot_general(
            both, flat_ref[runs[v]], (((0,), (0,)), ((), ())), preferred_element_type=F32
        ) * scale
        for q in range(2):
            keep, give = own_half(grads[q * lanes : (q + 1) * lanes], own_rows)
            span = pl.ds((2 * v + q) * width, width)
            keep_ref[:, span] = keep
            give_ref[:, span] = give

    peaks = []
    for v in range(clips):
        copies[v].wait()
        peaks.append(score(v))
    for v in range(clips):
        pool(v, peaks[v])


def caption_mean(row, lanes):
    row = jnp.broadcast_to(row, (8, lanes))
    lane = lax.broadcasted_iota(jnp.int32, (8, lanes), 1)
    step = 1
    while step < WORDS:
        up = pltpu.roll(row, lanes - step, 1)
        down = pltpu.roll(row, step, 1)
        row = row + jnp.where((lane & step) == 0, up, down)
        step *= 2
    return row * (1.0 / WORDS)


def merge(clips, stats, v):
    peaks = [s[pl.ds(v, 1)] for s in stats]
    totals = [s[pl.ds(clips + v, 1)] for s in stats]
    weighted = [s[pl.ds(2 * clips + v, 1)] for s in stats]
    peak = functools.reduce(jnp.maximum, peaks)
    factors = [jnp.exp(p - peak) for p in peaks]
    inverse = 1.0 / sum(f * t for f, t in zip(factors, totals))
    pooled = sum(f * w for f, w in zip(factors, weighted)) * inverse
    shares = [(f * inverse, w / t - pooled) for f, w, t in zip(factors, weighted, totals)]
    return peak, inverse, pooled, shares


def pair_order(mesh):
    places = [getattr(d, "coords", (n // 2,)) for n, d in enumerate(mesh.devices.flat)][::2]
    spans = [max(axis) + 1 for axis in zip(*places)]

    def apart(one, two):
        steps = [abs(a - b) for a, b in zip(one, two)]
        return sum(min(step, span - step) for step, span in zip(steps, spans))

    lead = max(places, key=lambda place: apart(place, places[0]))
    return sorted(range(len(places)), key=lambda pair: apart(places[pair], lead))


def pack_kernel(clips, shards, order, *refs):
    stats = refs[:shards]
    keep_ref, got_ref, send_ref = refs[shards:]
    pairs, own_rows, _ = send_ref.shape
    width = keep_ref.shape[1] // (2 * clips)
    lanes = stats[0].shape[1]
    group = WORDS // clips
    lane = lax.broadcasted_iota(jnp.int32, (8, lanes), 1)
    means = None
    columns = []
    for v in range(clips):
        _, _, pooled, shares = merge(clips, stats, v)
        mean = caption_mean(pooled, lanes)
        inside = (lane & (WORDS - 1)) >= v * group
        means = mean if means is None else jnp.where(inside, mean, means)
        for factor, shift in shares[:2]:
            columns += [factor, factor * shift]
    fill = -len(columns) % 8
    columns += [jnp.zeros((1, lanes), F32)] * fill
    columns, _ = own_half(jnp.concatenate(columns, axis=0).T, own_rows)
    for v in range(clips):
        out = None
        for n, ref in enumerate((keep_ref, got_ref)):
            for q in range(2):
                k = 4 * v + 2 * n + q
                term = columns[:, k : k + 1] * ref[:, pl.ds((2 * v + q) * width, width)]
                out = term if out is None else out + term
        out = out.reshape(pairs, own_rows, width).astype(BF16)
        for slot, pair in enumerate(order):
            send_ref[slot, :, pl.ds(v * width, width)] = out[pair]
    high = means.astype(BF16)
    rest = means - high.astype(F32)
    middle = rest.astype(BF16)
    low = (rest - middle.astype(F32)).astype(BF16)
    row = lax.broadcasted_iota(jnp.int32, (own_rows, lanes), 0)
    pieces = [p.astype(F32)[:1] for p in (high, middle, low)]
    block = jnp.where(row == 0, pieces[0], jnp.where(row == 1, pieces[1], jnp.where(row == 2, pieces[2], 0.0)))
    send_ref[:, :, pl.ds(clips * width, lanes)] = jnp.broadcast_to(
        block.astype(BF16)[None], (pairs, own_rows, lanes)
    )


def backward_kernel(
    clips, frame_max, shards, order, scale,
    got_ref, scores_ref, text_ref, *refs,
):
    stats = refs[:shards]
    loss_hbm, flat_grad_hbm, text_grad_hbm, staged_ref, loss_ref, text_grad_ref, sems = refs[shards:]
    lanes, width = text_ref.shape
    senders, own_rows, _ = got_ref.shape
    owners = lax.axis_size("clip")
    shares = senders // owners
    slots = [order.index(pair) for pair in range(senders)]
    clip_total = owners * clips
    group = WORDS // clips
    rank = lax.axis_index("clip")
    device = rank * shards + lax.axis_index("cap")
    lane = lax.broadcasted_iota(jnp.int32, (1, lanes), 1)
    word = lane & (WORDS - 1)
    rows = []
    for i in range(owners):
        pieces = got_ref[slots[i * shares], :, pl.ds(clips * width, lanes)].astype(F32)
        rows.append(pieces[0:1] + pieces[1:2] + pieces[2:3])
    packed = jnp.concatenate(rows, axis=0)
    by_clip = []
    for v in range(clips):
        mean = packed
        step = group
        while step < WORDS:
            up = pltpu.roll(mean, lanes - step, 1)
            down = pltpu.roll(mean, step, 1)
            keep = ((word & step) != 0) == ((v * group & step) != 0)
            mean = jnp.where(keep, mean, jnp.where((word & step) == 0, up, down))
            step *= 2
        by_clip.append(logit_scale * mean)
    owner = lax.broadcasted_iota(jnp.int32, (owners, lanes), 0)
    caption = lax.broadcasted_iota(jnp.int32, (owners, lanes), 1) // WORDS
    row_max = functools.reduce(jnp.maximum, [jnp.max(b, axis=0, keepdims=True) for b in by_clip])
    row_exp = [jnp.exp(b - row_max) for b in by_clip]
    row_sum = sum(jnp.sum(e, axis=0, keepdims=True) for e in row_exp)
    per_word = 1.0 / WORDS
    loss = jnp.sum(row_max + jnp.log(row_sum), axis=1, keepdims=True) * per_word
    factor = logit_scale / WORDS * loss_scale * 0.5 / clip_total
    grads = []
    for v in range(clips):
        col_max = jnp.max(by_clip[v], axis=1, keepdims=True)
        col_exp = jnp.exp(by_clip[v] - col_max)
        col_sum = jnp.sum(col_exp, axis=1, keepdims=True) * per_word
        same = caption == owner * clips + v
        loss += jnp.sum(col_max + jnp.log(col_sum), axis=0, keepdims=True)
        matched = jnp.where(same, by_clip[v], 0.0)
        loss -= 2.0 * per_word * jnp.sum(jnp.sum(matched, axis=1, keepdims=True), axis=0, keepdims=True)
        grads.append(
            factor * (row_exp[v] / row_sum + col_exp / col_sum - jnp.where(same, 2.0, 0.0))
        )
    loss_ref[...] = loss * (0.5 / clip_total)
    copies = [pltpu.make_async_copy(loss_ref, loss_hbm, sems.at[0])]
    copies[0].start()

    columns = scores_ref.shape[0] // clips
    parts = row_parts(columns, frame_max, BACKWARD_PARTS)
    for v in range(clips):
        mine = jnp.sum(jnp.where(owner == rank, grads[v], 0.0), axis=0, keepdims=True)
        peak, inverse, pooled, _ = merge(clips, stats, v)
        mine = mine * inverse
        for start, size in parts:
            run = pl.ds(v * columns + start, size)
            part = scores_ref[run]
            grad_scores = (mine * jnp.exp(part - peak) * (1.0 + part - pooled)).astype(BF16)
            staged_ref[run] = (
                jnp.dot(grad_scores, text_ref[...], preferred_element_type=F32) * scale
            ).astype(BF16)
            copy = pltpu.make_async_copy(
                staged_ref.at[run], flat_grad_hbm.at[run], sems.at[len(copies)]
            )
            copy.start()
            copies.append(copy)
    chosen = lax.broadcasted_iota(jnp.int32, (owners, lanes), 1) == device * own_rows
    out = jnp.zeros((own_rows, width), F32)
    for v in range(clips):
        column = jnp.sum(jnp.where(chosen, grads[v], 0.0), axis=1, keepdims=True)
        for i in range(owners):
            part = jnp.zeros((own_rows, width), F32)
            for k in range(shares):
                part += got_ref[slots[i * shares + k], :, pl.ds(v * width, width)].astype(F32)
            out += column[i : i + 1, :] * part
    text_grad_ref[...] = out
    copies.append(pltpu.make_async_copy(text_grad_ref, text_grad_hbm, sems.at[len(copies)]))
    copies[-1].start()
    for copy in copies:
        copy.wait()


def exchange(value, axis):
    size = lax.axis_size(axis)
    got = []
    for k in range(1, size):
        if size & (size - 1) == 0:
            pairs = [(i, i ^ k) for i in range(size)]
        else:
            pairs = [(i, (i + k) % size) for i in range(size)]
        got.append(lax.ppermute(value, axis, pairs))
    return got


def far(x):
    return pltpu.with_memory_space_constraint(x, pltpu.HBM)


def per_device(order, text, patches, frame_slots):
    clip_devices = lax.axis_size("clip")
    shards = lax.axis_size("cap")
    devices = clip_devices * shards
    clips, frame_max, patch_rows, width = patches.shape
    text_rows = text.shape[0]
    own_rows = text_rows // devices
    scale = width ** (-0.5)
    flat_rows = clips * patch_rows * frame_max
    pairs = devices // 2
    assert WORDS % own_rows == 0 and WORDS % clips == 0 and shards & (shards - 1) == 0
    assert shards > 1
    limit = pltpu.CompilerParams(vmem_limit_bytes=24 << 20)

    flat = patches.transpose(0, 2, 1, 3).reshape(flat_rows, width)
    stats, scores, text_near, give, keep = pl.pallas_call(
        functools.partial(forward_kernel, clips, frame_max, own_rows, scale),
        out_shape=(
            pltpu.VMEM((3 * clips, text_rows), F32),
            pltpu.VMEM((flat_rows, text_rows), F32),
            pltpu.VMEM((text_rows, width), BF16),
            pltpu.VMEM((text_rows // 2, 2 * clips * width), F32),
            pltpu.VMEM((text_rows // 2, 2 * clips * width), F32),
        ),
        in_specs=[ANY] * 3,
        out_specs=(VMEM,) * 5,
        scratch_shapes=[
            pltpu.VMEM((flat_rows, width), BF16),
            pltpu.SMEM(frame_slots.shape, jnp.int32),
            pltpu.SemaphoreType.DMA((clips + 2,)),
        ],
        compiler_params=limit,
        name="forward",
    )(far(text), far(flat), far(frame_slots))
    got = lax.ppermute(give, AXES, [(d, d ^ 1) for d in range(devices)])
    shares = [stats] + exchange(stats, "cap")
    sent = pl.pallas_call(
        functools.partial(pack_kernel, clips, shards, order),
        out_shape=pltpu.VMEM((pairs, own_rows, clips * width + text_rows), BF16),
        in_specs=[VMEM] * (shards + 2),
        out_specs=VMEM,
        compiler_params=limit,
        name="pack",
    )(*shares, keep, got)
    halves = [[2 * pair + side for pair in order] for side in range(2)]
    got = lax.all_to_all(
        sent, AXES, split_axis=0, concat_axis=0, tiled=True, axis_index_groups=halves
    )
    loss, flat_grad, text_grad = pl.pallas_call(
        functools.partial(backward_kernel, clips, frame_max, shards, order, scale),
        out_shape=(
            pltpu.HBM((1, 1), F32),
            pltpu.HBM((flat_rows, width), BF16),
            pltpu.HBM((own_rows, width), F32),
        ),
        in_specs=[VMEM] * (shards + 3),
        out_specs=(ANY, ANY, ANY),
        scratch_shapes=[
            pltpu.VMEM((flat_rows, width), BF16),
            pltpu.VMEM((1, 1), F32),
            pltpu.VMEM((own_rows, width), F32),
            pltpu.SemaphoreType.DMA((clips * BACKWARD_PARTS + 2,)),
        ],
        compiler_params=limit,
        name="backward",
    )(got, scores, text_near, *shares)
    patch_grad = flat_grad.reshape(clips, patch_rows, frame_max, width).transpose(0, 2, 1, 3)
    return (loss[0, 0], patch_grad, text_grad)


def solution(mesh):
    def step(*args):
        return per_device(order, *args)

    order = pair_order(mesh)
    return jax.shard_map(
        step,
        mesh=mesh,
        in_specs=(P(), P("clip", None, "cap", None), P("clip", None)),
        out_specs=(P(), P("clip", None, "cap", None), P(AXES, None)),
        check_vma=False,
    )
```

```python
import functools
import math

import jax
import jax.numpy as jnp
from jax import lax
from jax.experimental import pallas as pl
from jax.experimental.pallas import tpu as pltpu
from jax.sharding import PartitionSpec as P

WORDS = 8
AXES = ("clip", "cap")

logit_scale = 32.0
loss_scale = 8192.0
big_value = 1e30
LOG2E = math.log2(math.e)
LN2 = math.log(2.0)

F32 = jnp.float32
BF16 = jnp.bfloat16
ANY = pl.BlockSpec(memory_space=pl.ANY)
VMEM = pl.BlockSpec(memory_space=pltpu.VMEM)


BACKWARD_PARTS = 4
SCORE_PARTS = 2


def row_parts(columns, frame_max, parts):
    patch_rows = columns // frame_max
    edges = [patch_rows * k // parts * frame_max for k in range(parts + 1)]
    return [(a, b - a) for a, b in zip(edges, edges[1:])]


def valid_mask(slots_ref, v, frame_max, lanes):
    count = jnp.int32(0)
    for f in range(frame_max):
        count += (slots_ref[v, f] >= 0).astype(jnp.int32)
    return lax.broadcasted_iota(jnp.int32, (1, frame_max, lanes), 1) < count


def own_half(rows, own_rows):
    split = rows.reshape(-1, 2, own_rows, rows.shape[-1])
    even_rows = split[:, 0].reshape(-1, rows.shape[-1])
    odd_rows = split[:, 1].reshape(-1, rows.shape[-1])
    odd = (lax.axis_index("cap") & 1) == 1
    return jnp.where(odd, odd_rows, even_rows), jnp.where(odd, even_rows, odd_rows)


def forward_kernel(
    clips, frame_max, own_rows, scale,
    text_hbm, flat_hbm, slots_hbm,
    stats_ref, scores_ref, text_ref, give_ref, keep_ref,
    flat_ref, slots_ref, sems,
):
    columns, width = flat_ref.shape[0] // clips, flat_ref.shape[1]
    lanes = text_ref.shape[0]
    runs = [pl.ds(v * columns, columns) for v in range(clips)]
    copies = [
        pltpu.make_async_copy(flat_hbm.at[run], flat_ref.at[run], sems.at[v])
        for v, run in enumerate(runs)
    ]
    text_copy = pltpu.make_async_copy(text_hbm, text_ref, sems.at[clips])
    slots_copy = pltpu.make_async_copy(slots_hbm, slots_ref, sems.at[clips + 1])
    text_copy.start()
    slots_copy.start()
    for copy in copies:
        copy.start()
    slots_copy.wait()
    masks = [valid_mask(slots_ref, v, frame_max, lanes) for v in range(clips)]
    text_copy.wait()

    def score(v):
        peak = jnp.full((frame_max, lanes), -big_value, F32)
        for start, size in row_parts(columns, frame_max, SCORE_PARTS):
            run = pl.ds(v * columns + start, size)
            part = lax.dot_general(
                flat_ref[run], text_ref[...], (((1,), (1,)), ((), ())), preferred_element_type=F32
            ) * (scale * LOG2E)
            part = jnp.where(masks[v], part.reshape(-1, frame_max, lanes), -big_value)
            scores_ref[run] = part.reshape(-1, lanes)
            peak = jnp.maximum(peak, jnp.max(part, axis=0))
        return jnp.max(peak, axis=0, keepdims=True)

    def pool(v, peak):
        part = scores_ref[runs[v]].reshape(-1, frame_max, lanes)
        weight = jnp.exp2(part - peak[None])
        total = jnp.sum(jnp.sum(weight, axis=0), axis=0, keepdims=True)
        weighted = jnp.sum(jnp.sum(weight * part, axis=0), axis=0, keepdims=True)
        stats_ref[pl.ds(v, 1)] = peak
        stats_ref[pl.ds(clips + v, 1)] = total
        stats_ref[pl.ds(2 * clips + v, 1)] = weighted
        slope = weight * (part + (LOG2E - weighted / total)[None])
        both = jnp.concatenate(
            [slope.reshape(columns, lanes).astype(BF16), weight.reshape(columns, lanes).astype(BF16)],
            axis=1,
        )
        grads = lax.dot_general(
            both, flat_ref[runs[v]], (((0,), (0,)), ((), ())), preferred_element_type=F32
        ) * scale
        for q in range(2):
            keep, give = own_half(grads[q * lanes : (q + 1) * lanes], own_rows)
            span = pl.ds((2 * v + q) * width, width)
            keep_ref[:, span] = keep
            give_ref[:, span] = give

    peaks = []
    for v in range(clips):
        copies[v].wait()
        peaks.append(score(v))
    for v in range(clips):
        pool(v, peaks[v])


def caption_mean(row, lanes):
    row = jnp.broadcast_to(row, (8, lanes))
    lane = lax.broadcasted_iota(jnp.int32, (8, lanes), 1)
    step = 1
    while step < WORDS:
        up = pltpu.roll(row, lanes - step, 1)
        down = pltpu.roll(row, step, 1)
        row = row + jnp.where((lane & step) == 0, up, down)
        step *= 2
    return row * (1.0 / WORDS)


def merge(clips, stats, v):
    peaks = [s[pl.ds(v, 1)] for s in stats]
    totals = [s[pl.ds(clips + v, 1)] for s in stats]
    weighted = [s[pl.ds(2 * clips + v, 1)] for s in stats]
    peak = functools.reduce(jnp.maximum, peaks)
    factors = [jnp.exp2(p - peak) for p in peaks]
    inverse = 1.0 / sum(f * t for f, t in zip(factors, totals))
    pooled = sum(f * w for f, w in zip(factors, weighted)) * inverse
    shares = [(f * inverse, w / t - pooled) for f, w, t in zip(factors, weighted, totals)]
    return peak, inverse, pooled, shares


def pair_order(mesh):
    places = [getattr(d, "coords", (n // 2,)) for n, d in enumerate(mesh.devices.flat)][::2]
    spans = [max(axis) + 1 for axis in zip(*places)]

    def apart(one, two):
        steps = [abs(a - b) for a, b in zip(one, two)]
        return sum(min(step, span - step) for step, span in zip(steps, spans))

    lead = max(places, key=lambda place: apart(place, places[0]))
    return sorted(range(len(places)), key=lambda pair: apart(places[pair], lead))


def pack_kernel(clips, shards, order, *refs):
    stats = refs[:shards]
    keep_ref, got_ref, send_ref = refs[shards:]
    pairs, own_rows, _ = send_ref.shape
    width = keep_ref.shape[1] // (2 * clips)
    lanes = stats[0].shape[1]
    group = WORDS // clips
    lane = lax.broadcasted_iota(jnp.int32, (8, lanes), 1)
    means = None
    columns = []
    for v in range(clips):
        _, _, pooled, shares = merge(clips, stats, v)
        mean = caption_mean(pooled * LN2, lanes)
        inside = (lane & (WORDS - 1)) >= v * group
        means = mean if means is None else jnp.where(inside, mean, means)
        for factor, shift in shares[:2]:
            columns += [factor * LN2, factor * shift * LN2]
    fill = -len(columns) % 8
    columns += [jnp.zeros((1, lanes), F32)] * fill
    columns, _ = own_half(jnp.concatenate(columns, axis=0).T, own_rows)
    for v in range(clips):
        out = None
        for n, ref in enumerate((keep_ref, got_ref)):
            for q in range(2):
                k = 4 * v + 2 * n + q
                term = columns[:, k : k + 1] * ref[:, pl.ds((2 * v + q) * width, width)]
                out = term if out is None else out + term
        out = out.reshape(pairs, own_rows, width).astype(BF16)
        for slot, pair in enumerate(order):
            send_ref[slot, :, pl.ds(v * width, width)] = out[pair]
    high = means.astype(BF16)
    rest = means - high.astype(F32)
    middle = rest.astype(BF16)
    low = (rest - middle.astype(F32)).astype(BF16)
    row = lax.broadcasted_iota(jnp.int32, (own_rows, lanes), 0)
    pieces = [p.astype(F32)[:1] for p in (high, middle, low)]
    block = jnp.where(row == 0, pieces[0], jnp.where(row == 1, pieces[1], jnp.where(row == 2, pieces[2], 0.0)))
    send_ref[:, :, pl.ds(clips * width, lanes)] = jnp.broadcast_to(
        block.astype(BF16)[None], (pairs, own_rows, lanes)
    )


def backward_kernel(
    clips, frame_max, shards, order, scale,
    got_ref, scores_ref, text_ref, *refs,
):
    stats = refs[:shards]
    loss_hbm, flat_grad_hbm, text_grad_hbm, staged_ref, loss_ref, text_grad_ref, sems = refs[shards:]
    lanes, width = text_ref.shape
    senders, own_rows, _ = got_ref.shape
    owners = lax.axis_size("clip")
    shares = senders // owners
    slots = [order.index(pair) for pair in range(senders)]
    clip_total = owners * clips
    group = WORDS // clips
    rank = lax.axis_index("clip")
    device = rank * shards + lax.axis_index("cap")
    lane = lax.broadcasted_iota(jnp.int32, (1, lanes), 1)
    word = lane & (WORDS - 1)
    rows = []
    for i in range(owners):
        pieces = got_ref[slots[i * shares], :, pl.ds(clips * width, lanes)].astype(F32)
        rows.append(pieces[0:1] + pieces[1:2] + pieces[2:3])
    packed = jnp.concatenate(rows, axis=0)
    by_clip = []
    for v in range(clips):
        mean = packed
        step = group
        while step < WORDS:
            up = pltpu.roll(mean, lanes - step, 1)
            down = pltpu.roll(mean, step, 1)
            keep = ((word & step) != 0) == ((v * group & step) != 0)
            mean = jnp.where(keep, mean, jnp.where((word & step) == 0, up, down))
            step *= 2
        by_clip.append(logit_scale * mean)
    owner = lax.broadcasted_iota(jnp.int32, (owners, lanes), 0)
    caption = lax.broadcasted_iota(jnp.int32, (owners, lanes), 1) // WORDS
    row_max = functools.reduce(jnp.maximum, [jnp.max(b, axis=0, keepdims=True) for b in by_clip])
    row_exp = [jnp.exp(b - row_max) for b in by_clip]
    row_sum = sum(jnp.sum(e, axis=0, keepdims=True) for e in row_exp)
    per_word = 1.0 / WORDS
    loss = jnp.sum(row_max + jnp.log(row_sum), axis=1, keepdims=True) * per_word
    factor = logit_scale / WORDS * loss_scale * 0.5 / clip_total
    grads = []
    for v in range(clips):
        col_max = jnp.max(by_clip[v], axis=1, keepdims=True)
        col_exp = jnp.exp(by_clip[v] - col_max)
        col_sum = jnp.sum(col_exp, axis=1, keepdims=True) * per_word
        same = caption == owner * clips + v
        loss += jnp.sum(col_max + jnp.log(col_sum), axis=0, keepdims=True)
        matched = jnp.where(same, by_clip[v], 0.0)
        loss -= 2.0 * per_word * jnp.sum(jnp.sum(matched, axis=1, keepdims=True), axis=0, keepdims=True)
        grads.append(
            factor * (row_exp[v] / row_sum + col_exp / col_sum - jnp.where(same, 2.0, 0.0))
        )
    loss_ref[...] = loss * (0.5 / clip_total)
    copies = [pltpu.make_async_copy(loss_ref, loss_hbm, sems.at[0])]
    copies[0].start()

    columns = scores_ref.shape[0] // clips
    parts = row_parts(columns, frame_max, BACKWARD_PARTS)
    for v in range(clips):
        mine = jnp.sum(jnp.where(owner == rank, grads[v], 0.0), axis=0, keepdims=True)
        peak, inverse, pooled, _ = merge(clips, stats, v)
        mine = mine * (inverse * LN2)
        level = LOG2E - pooled
        for start, size in parts:
            run = pl.ds(v * columns + start, size)
            part = scores_ref[run]
            grad_scores = (mine * jnp.exp2(part - peak) * (part + level)).astype(BF16)
            staged_ref[run] = (
                jnp.dot(grad_scores, text_ref[...], preferred_element_type=F32) * scale
            ).astype(BF16)
            copy = pltpu.make_async_copy(
                staged_ref.at[run], flat_grad_hbm.at[run], sems.at[len(copies)]
            )
            copy.start()
            copies.append(copy)
    chosen = lax.broadcasted_iota(jnp.int32, (owners, lanes), 1) == device * own_rows
    out = jnp.zeros((own_rows, width), F32)
    for v in range(clips):
        column = jnp.sum(jnp.where(chosen, grads[v], 0.0), axis=1, keepdims=True)
        for i in range(owners):
            part = jnp.zeros((own_rows, width), F32)
            for k in range(shares):
                part += got_ref[slots[i * shares + k], :, pl.ds(v * width, width)].astype(F32)
            out += column[i : i + 1, :] * part
    text_grad_ref[...] = out
    copies.append(pltpu.make_async_copy(text_grad_ref, text_grad_hbm, sems.at[len(copies)]))
    copies[-1].start()
    for copy in copies:
        copy.wait()


def exchange(value, axis):
    size = lax.axis_size(axis)
    got = []
    for k in range(1, size):
        if size & (size - 1) == 0:
            pairs = [(i, i ^ k) for i in range(size)]
        else:
            pairs = [(i, (i + k) % size) for i in range(size)]
        got.append(lax.ppermute(value, axis, pairs))
    return got


def far(x):
    return pltpu.with_memory_space_constraint(x, pltpu.HBM)


def per_device(order, text, patches, frame_slots):
    clip_devices = lax.axis_size("clip")
    shards = lax.axis_size("cap")
    devices = clip_devices * shards
    clips, frame_max, patch_rows, width = patches.shape
    text_rows = text.shape[0]
    own_rows = text_rows // devices
    scale = width ** (-0.5)
    flat_rows = clips * patch_rows * frame_max
    pairs = devices // 2
    assert WORDS % own_rows == 0 and WORDS % clips == 0 and shards & (shards - 1) == 0
    assert shards > 1
    limit = pltpu.CompilerParams(vmem_limit_bytes=24 << 20)

    flat = patches.transpose(0, 2, 1, 3).reshape(flat_rows, width)
    stats, scores, text_near, give, keep = pl.pallas_call(
        functools.partial(forward_kernel, clips, frame_max, own_rows, scale),
        out_shape=(
            pltpu.VMEM((3 * clips, text_rows), F32),
            pltpu.VMEM((flat_rows, text_rows), F32),
            pltpu.VMEM((text_rows, width), BF16),
            pltpu.VMEM((text_rows // 2, 2 * clips * width), F32),
            pltpu.VMEM((text_rows // 2, 2 * clips * width), F32),
        ),
        in_specs=[ANY] * 3,
        out_specs=(VMEM,) * 5,
        scratch_shapes=[
            pltpu.VMEM((flat_rows, width), BF16),
            pltpu.SMEM(frame_slots.shape, jnp.int32),
            pltpu.SemaphoreType.DMA((clips + 2,)),
        ],
        compiler_params=limit,
        name="forward",
    )(far(text), far(flat), far(frame_slots))
    got = lax.ppermute(give, AXES, [(d, d ^ 1) for d in range(devices)])
    shares = [stats] + exchange(stats, "cap")
    sent = pl.pallas_call(
        functools.partial(pack_kernel, clips, shards, order),
        out_shape=pltpu.VMEM((pairs, own_rows, clips * width + text_rows), BF16),
        in_specs=[VMEM] * (shards + 2),
        out_specs=VMEM,
        compiler_params=limit,
        name="pack",
    )(*shares, keep, got)
    halves = [[2 * pair + side for pair in order] for side in range(2)]
    got = lax.all_to_all(
        sent, AXES, split_axis=0, concat_axis=0, tiled=True, axis_index_groups=halves
    )
    loss, flat_grad, text_grad = pl.pallas_call(
        functools.partial(backward_kernel, clips, frame_max, shards, order, scale),
        out_shape=(
            pltpu.HBM((1, 1), F32),
            pltpu.HBM((flat_rows, width), BF16),
            pltpu.HBM((own_rows, width), F32),
        ),
        in_specs=[VMEM] * (shards + 3),
        out_specs=(ANY, ANY, ANY),
        scratch_shapes=[
            pltpu.VMEM((flat_rows, width), BF16),
            pltpu.VMEM((1, 1), F32),
            pltpu.VMEM((own_rows, width), F32),
            pltpu.SemaphoreType.DMA((clips * BACKWARD_PARTS + 2,)),
        ],
        compiler_params=limit,
        name="backward",
    )(got, scores, text_near, *shares)
    patch_grad = flat_grad.reshape(clips, patch_rows, frame_max, width).transpose(0, 2, 1, 3)
    return (loss[0, 0], patch_grad, text_grad)


def solution(mesh):
    def step(*args):
        return per_device(order, *args)

    order = pair_order(mesh)
    return jax.shard_map(
        step,
        mesh=mesh,
        in_specs=(P(), P("clip", None, "cap", None), P("clip", None)),
        out_specs=(P(), P("clip", None, "cap", None), P(AXES, None)),
        check_vma=False,
    )
```
